32 devices in a mesh: seq: 8 (over z, x), mp: 4 (over y, core).
Axes of the slice: x: 2, y: 2, z: 4, core: 2. Of those that a mesh axis runs over, the one named last changes fastest.
Arguments:
- patches: bfloat16 [8192, 1280], P('seq'), may hold values from -6 to 6
- clip_of: int32 [8192, 1], P('seq'), may hold values from 0 to 7; in each aligned block of 1024 rows (0 to 1023, 1024 to 2047, ...) at most 256 rows name the same one
- owner_of: int32 [8], replicated, may hold values from 0 to 7, each once
- cites: int32 [256, 4], P('seq'), may hold values from 0 to 7, all different within a row; in each aligned block of 32 rows (0 to 31, 32 to 63, ...) at most 32 rows name the same one
- latent_init: bfloat16 [64, 1280], replicated
- w_query: bfloat16 [1280, 1280], P(None, 'mp'), may hold values from -0.15625 to 0.15625
- w_key: bfloat16 [1280, 1280], P(None, 'mp'), may hold values from -0.15625 to 0.15625
- w_value: bfloat16 [1280, 1280], P(None, 'mp'), may hold values from -0.15625 to 0.15625
- w_out: bfloat16 [1280, 1280], P('mp'), may hold values from -0.15625 to 0.15625
- wx_key: bfloat16 [1280, 4096], P(None, 'mp'), may hold values from -0.15625 to 0.15625
- wx_value: bfloat16 [1280, 4096], P(None, 'mp'), may hold values from -0.15625 to 0.15625
- queries: bfloat16 [4096, 4096], P('seq', 'mp')
Outputs:
- resampled: bfloat16 [512, 1280], P('seq')
- context: bfloat16 [4096, 4096], P('seq', 'mp')
The draws below stay inside these ranges and needn't reach their ends.
Inputs may be any that keep to these rules, and one draw needn't show every extreme that they name: `clip_of`: within the 1024 patch rows of one index of seq at most 256 name the same clip, and some clip reaches 256. `owner_of`: each index of seq owns exactly one clip. A question cites 4 different clips; among the 32 questions of one index of seq no clip is cited more than 32 times, and some clip reaches 32.
All inputs are finite; a program needn't handle non-finite values.
Results may differ from the reference program's by a relative error of at most 0.023.
The reference program's roundings to bfloat16 on the way count: a program that leaves them out, or rounds other values in their place, can miss the bound.
Values may be sent and summed in bfloat16 or wider, within the bound.
No kernel may reach another device: no remote copies, remote signals or barrier semaphores. Data moves between devices by JAX's collectives and lax.ppermute only.
A program may use at most 128 MiB of HBM per device.

```python
import math
import jax
import jax.numpy as jnp
import numpy as np
from jax import lax

DV = 1280
RH = 16
RHD = 80
LAT = 64
HX = 32
HD = 128
CITE = 4
TQ = 16
P_DEV = 1024
Q_DEV = 32
CLIPS = 8
PATCHES = 8192
QUESTIONS = 256
TOKENS = 4096
CAP = 256
MOSTQ = 32
LATROWS = 512
XW = 4096


def draw_latent_init(key, part):
    base = jax.random.normal(key, (LAT, DV), jnp.float32)
    return base.astype(jnp.bfloat16)


def draw_queries(key, part):
    base = jax.random.normal(key, (TOKENS, XW), jnp.float32)
    return base.astype(jnp.bfloat16)


def shard_levels(rng, dims, split, least, top_value):
    level, own = 1.0, jax.random.fold_in(rng, 6)
    for dim, blocks in split:
        draws = jnp.exp(jax.random.uniform(jax.random.fold_in(own, dim), (blocks,), jnp.float32, least / len(split), top_value / len(split)))
        level = level * jnp.repeat(draws, dims[dim] // blocks).reshape([-1 if axis == dim else 1 for axis in range(len(dims))])
    return level


def routed_block(stream_key, own, number, rows, amount, top, limit, skew):
    sequence = jax.random.permutation(stream_key, amount)
    heavy_load, ordinary = shares(amount, rows * top, limit, skew, True), shares(amount, rows * top, limit, skew, False)
    places = jnp.arange(amount)

    def named(tallies, rotation):
        used = int((tallies > 0).sum())
        fixed = max(1, used // 4)
        shifted = fixed + (places - fixed + rotation * (used - fixed)) % max(1, amount - fixed)
        return jnp.zeros((amount,), jnp.int32).at[sequence[jnp.where(places < fixed, places, shifted)]].set(jnp.asarray(tallies, jnp.int32))

    tallies = jnp.where(number % 4 == 0, named(heavy_load, number // 4), named(ordinary, number - number // 4 - 1))
    mixed = jax.random.permutation(jax.random.fold_in(own, 3), amount)
    source_of, taker = mixed[0:amount // 2 * 2:2], mixed[1:amount // 2 * 2:2]
    slack = jnp.minimum(tallies[source_of] - 1, limit - tallies[taker]) // 2
    slack = jnp.where((source_of == sequence[0]) | (taker == sequence[0]) | (tallies[taker] == 0), 0, jnp.maximum(slack, 0))
    shifted = jax.random.randint(jax.random.fold_in(own, 4), (amount // 2,), 0, 1 << 20) % (slack + 1)
    tallies = tallies.at[source_of].add(-shifted).at[taker].add(shifted)
    members = jnp.searchsorted(jnp.cumsum(tallies), jnp.arange(rows * top), side="right").astype(jnp.int32)
    grid = members.reshape(top, rows).T
    grid = grid[jax.random.permutation(jax.random.fold_in(own, 1), rows)]
    rotation = jax.random.randint(jax.random.fold_in(own, 2), (rows, 1), 0, top)
    return jnp.take_along_axis(grid, (jnp.arange(top)[None, :] + rotation) % top, axis=1)


def shares(count, total, reach, slope, full):
    loads = [(1 << 20) // math.isqrt(rank ** slope) + 1 for rank in range(1, count + 1)]
    largest = reach if full else min(reach, max(-(-total // count), total * loads[0] // sum(loads)))
    least = 1 if total - largest >= count - 1 else 0
    given, rest = [largest] + [least] * (count - 1), total - largest - least * (count - 1)
    while rest > 0:
        candidates = [i for i in range(1, count) if given[i] < largest] or [i for i in range(1, count) if given[i] < reach]
        whole, remaining = sum([loads[i] for i in candidates]), rest
        for i in candidates:
            more = min(reach - given[i], max(1, remaining * loads[i] // whole), rest)
            given[i] = given[i] + more
            rest = rest - more
    return np.array(given)


def centred(key, shape, spread, limit, shards=(), held_as=jnp.bfloat16):
    drawn = jax.random.normal(key, shape, jnp.float32) * spread
    if len(shards) > 0:
        drawn = shard_levels(key, shape, shards, -0.22, 0.18) * drawn
    return jnp.clip(drawn, min=-limit, max=limit).astype(held_as)


def setup_inputs(seed: int = 0) -> dict:
    key_list = jax.random.split(jax.random.key(seed), 13)
    patches = centred(key_list[0], (PATCHES, DV), 1.0, 6.0, ((0, 8),))
    clip_of_keys = jax.random.split(jax.random.fold_in(key_list[1], 1), PATCHES // P_DEV)
    clip_of_turns = jax.random.permutation(jax.random.fold_in(key_list[1], 3), PATCHES // P_DEV)
    clip_of = jax.vmap(lambda own, number: routed_block(jax.random.fold_in(key_list[1], 2), own, number, P_DEV, CLIPS, 1, CAP, 2))(clip_of_keys, clip_of_turns).reshape((PATCHES, 1))
    owner_of = jax.random.permutation(key_list[2], CLIPS).astype(jnp.int32)
    cites_keys = jax.random.split(jax.random.fold_in(key_list[3], 1), QUESTIONS // Q_DEV)
    cites_turns = jax.random.permutation(jax.random.fold_in(key_list[3], 3), QUESTIONS // Q_DEV)
    cites = jax.vmap(lambda own, number: routed_block(jax.random.fold_in(key_list[3], 2), own, number, Q_DEV, CLIPS, CITE, MOSTQ, 1))(cites_keys, cites_turns).reshape((QUESTIONS, CITE))
    latent_init = draw_latent_init(jax.random.fold_in(key_list[12], 71), 0)
    w_query = centred(key_list[5], (DV, DV), DV ** -0.5, 0.15625, ((1, 4),))
    w_key = centred(key_list[6], (DV, DV), DV ** -0.5, 0.15625, ((1, 4),))
    w_value = centred(key_list[7], (DV, DV), DV ** -0.5, 0.15625, ((1, 4),))
    w_out = centred(key_list[8], (DV, DV), DV ** -0.5, 0.15625, ((0, 4),))
    wx_key = centred(key_list[9], (DV, XW), DV ** -0.5, 0.15625, ((1, 4),))
    wx_value = centred(key_list[10], (DV, XW), DV ** -0.5, 0.15625, ((1, 4),))
    queries = draw_queries(jax.random.fold_in(key_list[12], 71), 0)
    return dict(patches=patches, clip_of=clip_of, owner_of=owner_of, cites=cites, latent_init=latent_init, w_query=w_query, w_key=w_key, w_value=w_value, w_out=w_out, wx_key=wx_key, wx_value=wx_value, queries=queries)


masked_score = -1e+30

def reference(patches, clip_of, owner_of, cites, latent_init, w_query, w_key, w_value, w_out, wx_key, wx_value, queries):
    patch_keys = jnp.dot(patches, w_key, preferred_element_type=jnp.float32).astype(jnp.bfloat16)
    patch_values = jnp.dot(patches, w_value, preferred_element_type=jnp.float32).astype(jnp.bfloat16)
    latent_query = jnp.dot(latent_init, w_query, preferred_element_type=jnp.float32).astype(jnp.bfloat16)
    latent_keys = jnp.dot(latent_init, w_key, preferred_element_type=jnp.float32).astype(jnp.bfloat16)
    latent_values = jnp.dot(latent_init, w_value, preferred_element_type=jnp.float32).astype(jnp.bfloat16)
    query_heads = latent_query.astype(jnp.float32).reshape(LAT, RH, RHD)
    key_heads = patch_keys.astype(jnp.float32).reshape(PATCHES, RH, RHD)
    value_heads = patch_values.astype(jnp.float32).reshape(PATCHES, RH, RHD)
    lat_key_heads = latent_keys.astype(jnp.float32).reshape(LAT, RH, RHD)
    lat_value_heads = latent_values.astype(jnp.float32).reshape(LAT, RH, RHD)
    clip_ids = clip_of[:, 0]
    clip_hot = (clip_ids[:, None] == jnp.arange(CLIPS, dtype=jnp.int32)[None, :]).astype(jnp.int32)
    counts = lax.optimization_barrier(jnp.sum(clip_hot, axis=0))
    starts = jnp.cumsum(counts) - counts
    span = CLIPS * CAP
    order = jnp.argsort(clip_ids, stable=True).astype(jnp.int32)
    order_pad = jnp.concatenate([order, jnp.zeros((span,), jnp.int32)])
    inv_scale = 1.0 / math.sqrt(RHD)
    latent_scores = jnp.einsum('qhd,khd->hqk', query_heads, lat_key_heads) * inv_scale

    def one_clip(clip_id):
        picked = lax.dynamic_slice(order_pad, (starts[clip_id].astype(jnp.int32),), (span,))
        live_slots = jnp.arange(span, dtype=jnp.int32) < counts[clip_id]
        keys_here = key_heads[picked]
        values_here = value_heads[picked]
        patch_scores = jnp.einsum('qhd,khd->hqk', query_heads, keys_here) * inv_scale
        patch_scores = jnp.where(live_slots[None, None, :], patch_scores, masked_score)
        row_max = jnp.maximum(lax.optimization_barrier(jnp.max(patch_scores, axis=-1)), lax.optimization_barrier(jnp.max(latent_scores, axis=-1)))
        patch_raised = jnp.exp(patch_scores - row_max[..., None])
        latent_raised = jnp.exp(latent_scores - row_max[..., None])
        row_sum = lax.optimization_barrier(jnp.sum(patch_raised, axis=-1)) + lax.optimization_barrier(jnp.sum(latent_raised, axis=-1))
        patch_weights = (patch_raised / row_sum[..., None]).astype(jnp.bfloat16)
        latent_weights = (latent_raised / row_sum[..., None]).astype(jnp.bfloat16)
        patch_weights = lax.optimization_barrier(patch_weights).astype(jnp.float32)
        latent_weights = lax.optimization_barrier(latent_weights).astype(jnp.float32)
        mixed_heads = jnp.einsum('hqk,khd->qhd', patch_weights, values_here)
        mixed_heads = mixed_heads + jnp.einsum('hqk,khd->qhd', latent_weights, lat_value_heads)
        mixed_heads = mixed_heads.astype(jnp.bfloat16).reshape(LAT, DV)
        projected = jnp.dot(mixed_heads, w_out, preferred_element_type=jnp.float32)
        return (latent_init.astype(jnp.float32) + projected).astype(jnp.bfloat16)
    clip_latents = lax.map(one_clip, jnp.arange(CLIPS, dtype=jnp.int32))
    flat_latents = clip_latents.reshape(CLIPS * LAT, DV)
    cross_keys = jnp.dot(flat_latents, wx_key, preferred_element_type=jnp.float32).astype(jnp.bfloat16).reshape(CLIPS, LAT, HX, HD)
    cross_values = jnp.dot(flat_latents, wx_value, preferred_element_type=jnp.float32).astype(jnp.bfloat16).reshape(CLIPS, LAT, HX, HD)
    query_rows = queries.astype(jnp.float32).reshape(QUESTIONS, TQ, HX, HD)
    inv_cross = 1.0 / math.sqrt(HD)
    maxima = []
    totals = []
    partials = []
    for cite_pos in range(CITE):
        picked = cites[:, cite_pos]
        keys_here = cross_keys[picked].astype(jnp.float32)
        values_here = cross_values[picked].astype(jnp.float32)
        scores = jnp.einsum('bthd,bkhd->bthk', query_rows, keys_here) * inv_cross
        row_max = lax.optimization_barrier(jnp.max(scores, axis=-1))
        raised = jnp.exp(scores - row_max[..., None])
        totals.append(lax.optimization_barrier(jnp.sum(raised, axis=-1)))
        weights = lax.optimization_barrier(raised.astype(jnp.bfloat16)).astype(jnp.float32)
        partials.append(jnp.einsum('bthk,bkhd->bthd', weights, values_here).astype(jnp.bfloat16))
        maxima.append(row_max)
    maxima = jnp.stack(maxima)
    totals = jnp.stack(totals)
    partials = jnp.stack(partials)
    best_max = lax.optimization_barrier(jnp.max(maxima, axis=0))
    rescale = jnp.exp(maxima - best_max[None])
    denominator = lax.optimization_barrier(jnp.sum(rescale * totals, axis=0))
    numerator = lax.optimization_barrier(jnp.sum(rescale[..., None] * partials.astype(jnp.float32), axis=0))
    context = (numerator / denominator[..., None]).astype(jnp.bfloat16).reshape(TOKENS, XW)
    resampled = jnp.zeros_like(clip_latents).at[owner_of].set(clip_latents).reshape(LATROWS, DV)
    return (resampled, context)
```

```python
import math

import jax
import jax.numpy as jnp
from jax import lax
from jax.sharding import PartitionSpec as P

RHD = 80
LAT = 64
HD = 128

masked_score = -1e30


def split3(x):
    a = x.astype(jnp.bfloat16)
    r = x - a.astype(jnp.float32)
    b = r.astype(jnp.bfloat16)
    c = (r - b.astype(jnp.float32)).astype(jnp.bfloat16)
    return a, b, c


def gather_axis(x, name):
    count = lax.axis_size(name)
    if count & (count - 1):
        return lax.all_gather(x, name, axis=0)
    me = lax.axis_index(name)
    x = x[None]
    step = count // 2
    while step >= 1:
        other = lax.ppermute(x, name, [(i, i ^ step) for i in range(count)])
        low = (me & step) == 0
        x = jnp.where(low, jnp.stack([x, other]), jnp.stack([other, x]))
        x = x.reshape((-1,) + x.shape[2:])
        step //= 2
    bits = count.bit_length() - 1
    order = [int(format(i, "0%db" % bits)[::-1], 2) if bits else 0 for i in range(count)]
    return jnp.stack([x[order[i]] for i in range(count)])


def body(
    patches,
    clip_of,
    owner_of,
    cites,
    latent_init,
    w_query,
    w_key,
    w_value,
    w_out,
    wx_key,
    wx_value,
    queries,
):
    groups = lax.axis_size("seq")
    clip_total = owner_of.shape[0]
    rows = patches.shape[0]
    f32, bf16 = jnp.float32, jnp.bfloat16

    w_out_all = gather_axis(w_out, "mp").reshape(-1, w_out.shape[1])

    clip_hot = (clip_of == jnp.arange(clip_total, dtype=jnp.int32)[None, :]).astype(jnp.int32)
    target = jnp.sum(clip_hot * owner_of[None, :], axis=1)
    key_rows = jnp.dot(patches, w_key, preferred_element_type=f32).astype(bf16)
    value_rows = jnp.dot(patches, w_value, preferred_element_type=f32).astype(bf16)
    lat_q = jnp.dot(latent_init, w_query, preferred_element_type=f32).astype(bf16)
    lat_k = jnp.dot(latent_init, w_key, preferred_element_type=f32).astype(bf16)
    lat_v = jnp.dot(latent_init, w_value, preferred_element_type=f32).astype(bf16)
    heads = lat_q.shape[1] // RHD
    q = lat_q.reshape(LAT, heads, RHD)

    scale = 1.0 / math.sqrt(RHD)
    scores = (
        jnp.einsum("qhd,khd->hqk", q, key_rows.reshape(rows, heads, RHD), preferred_element_type=f32)
        * scale
    )
    member = target[None, :] == jnp.arange(groups, dtype=jnp.int32)[:, None]
    peak = jnp.max(
        jnp.where(member[:, None, None, :], scores[None], masked_score), axis=-1
    )
    raised = jnp.where(
        member[:, None, None, :], jnp.exp(scores[None] - peak[..., None]), 0.0
    )
    total = jnp.sum(raised, axis=-1)
    out = jnp.einsum(
        "ghqk,khd->gqhd",
        raised.astype(bf16),
        value_rows.reshape(rows, heads, RHD),
        preferred_element_type=f32,
    )
    safe = jnp.where(total > 0, total, 1.0)
    out = out / jnp.swapaxes(safe, 1, 2)[..., None]
    lse = jnp.where(total > 0, peak + jnp.log(safe), masked_score)
    lse = jnp.swapaxes(lse, 1, 2)
    pad = 384 - heads * RHD - 3 * heads
    packed = jnp.concatenate(
        [out.reshape(groups, LAT, heads * RHD).astype(bf16)]
        + list(split3(lse))
        + [jnp.zeros((groups, LAT, pad), bf16)],
        axis=-1,
    )
    got = lax.all_to_all(packed, "seq", split_axis=0, concat_axis=0, tiled=True)
    width = heads * RHD
    got_out = got[..., :width].astype(f32).reshape(groups, LAT, heads, RHD)
    tail = got[..., width : width + 3 * heads].astype(f32).reshape(groups, LAT, 3, heads)
    got_lse = tail[:, :, 0] + tail[:, :, 1] + tail[:, :, 2]

    lat_scores = (
        jnp.einsum("qhd,khd->qhk", q, lat_k.reshape(LAT, heads, RHD), preferred_element_type=f32)
        * scale
    )
    lat_peak = jnp.max(lat_scores, axis=-1)
    lat_raised = jnp.exp(lat_scores - lat_peak[..., None])
    lat_total = jnp.sum(lat_raised, axis=-1)
    lat_out = jnp.einsum(
        "qhk,khd->qhd",
        lat_raised.astype(bf16),
        lat_v.reshape(LAT, heads, RHD),
        preferred_element_type=f32,
    )
    best = jnp.maximum(jnp.max(got_lse, axis=0), lat_peak)
    lat_w = jnp.exp(lat_peak - best)
    part_w = jnp.exp(got_lse - best[None])
    denominator = lat_w * lat_total + jnp.sum(part_w, axis=0)
    numerator = lat_w[..., None] * lat_out + jnp.sum(part_w[..., None] * got_out, axis=0)
    mixed = (numerator / denominator[..., None]).astype(bf16).reshape(LAT, width)

    mixed_all = gather_axis(gather_axis(mixed, "seq"), "mp")
    mixed_all = jnp.moveaxis(mixed_all, 0, 2).reshape(groups * LAT, -1)
    latents = jnp.dot(mixed_all, w_out_all, preferred_element_type=f32)
    latents = latents.reshape(groups, LAT, -1) + latent_init.astype(f32)[None]
    latents = latents.astype(bf16)
    resampled = lax.dynamic_index_in_dim(latents, lax.axis_index("seq"), 0, keepdims=False)
    latents = latents.reshape(groups * LAT, -1)

    cross_keys = jnp.dot(latents, wx_key, preferred_element_type=f32).astype(bf16)
    cross_values = jnp.dot(latents, wx_value, preferred_element_type=f32).astype(bf16)
    cross_heads = cross_keys.shape[1] // HD
    question_count = cites.shape[0]
    question_len = queries.shape[0] // question_count
    cite_hot = cites[:, :, None] == jnp.arange(clip_total, dtype=jnp.int32)[None, None, :]
    cite_owner = jnp.sum(cite_hot * owner_of[None, None, :], axis=2)
    cited = jnp.any(
        cite_owner[:, :, None] == jnp.arange(groups, dtype=jnp.int32)[None, None, :], axis=1
    )
    token_cited = jnp.repeat(cited, question_len, axis=0)
    key_cited = jnp.repeat(token_cited, LAT, axis=1)
    q_heads = queries.reshape(-1, cross_heads, HD)
    s = jnp.einsum(
        "thd,khd->htk", q_heads, cross_keys.reshape(-1, cross_heads, HD), preferred_element_type=f32
    ) * (1.0 / math.sqrt(HD))
    s = jnp.where(key_cited[None], s, masked_score)
    top = jnp.max(s, axis=-1, keepdims=True)
    p = jnp.exp(s - top)
    denom = jnp.sum(p, axis=-1)
    ctx = jnp.einsum(
        "htk,khd->thd",
        p.astype(bf16),
        cross_values.reshape(-1, cross_heads, HD),
        preferred_element_type=f32,
    )
    ctx = ctx / denom.T[..., None]
    return (resampled, ctx.astype(bf16).reshape(queries.shape))


def solution(mesh):
    in_specs = (
        P("seq", None),
        P("seq", None),
        P(),
        P("seq", None),
        P(),
        P(None, "mp"),
        P(None, "mp"),
        P(None, "mp"),
        P("mp", None),
        P(None, "mp"),
        P(None, "mp"),
        P("seq", "mp"),
    )
    out_specs = (P("seq", None), P("seq", "mp"))
    return jax.shard_map(body, mesh=mesh, in_specs=in_specs, out_specs=out_specs, check_vma=False)
```

```python
import functools
import math

import jax
import jax.numpy as jnp
from jax import lax
from jax.experimental import pallas as pl
from jax.experimental.pallas import tpu as pltpu
from jax.sharding import PartitionSpec as P

RHD = 80
LAT = 64
HD = 128
KEYS = 512

masked_score = -1e30
f32 = jnp.float32
bf16 = jnp.bfloat16


def matmul(a, b):
    return jnp.dot(a, b, preferred_element_type=f32)


def matmul_nt(a, b):
    return lax.dot_general(a, b, (((1,), (1,)), ((), ())), preferred_element_type=f32)


def split3(x):
    a = x.astype(bf16).astype(f32)
    b = (x - a).astype(bf16).astype(f32)
    return a, b, x - a - b


def finish(out, peak, total, heads):
    safe = jnp.where(total > 0, total, 1.0)
    lse = jnp.where(total > 0, peak + jnp.log(safe), masked_score)
    cols = [out[h] / safe[h * LAT : (h + 1) * LAT] for h in range(heads)]
    for part in split3(lse):
        cols += [part[h * LAT : (h + 1) * LAT] for h in range(heads)]
    cols.append(jnp.zeros((LAT, 384 - heads * (RHD + 3)), f32))
    return jnp.concatenate(cols, axis=1)


def partial_kernel(
    owner_ref, clip_ref, patches_ref, lat_ref, wq_ref, wk_ref, wv_ref,
    out_ref, lat_out_ref, qbd, scores, values, masked, peaks,
):
    step = pl.program_id(0)
    block = patches_ref.shape[0]
    width = wq_ref.shape[1]
    heads = width // RHD
    clips = owner_ref.shape[0]
    scale = 1.0 / math.sqrt(RHD)

    @pl.when(step == 0)
    def _():
        lat = lat_ref[...]
        q = matmul(lat, wq_ref[...])
        lane = lax.broadcasted_iota(jnp.int32, q.shape, 1)
        for h in range(heads):
            inside = (lane >= h * RHD) & (lane < (h + 1) * RHD)
            qbd[h * LAT : (h + 1) * LAT, :] = jnp.where(inside, q, 0.0).astype(bf16)
        lk = matmul(lat, wk_ref[...]).astype(bf16)
        lv = matmul(lat, wv_ref[...]).astype(bf16)
        s = matmul_nt(qbd[...], lk) * scale
        peak = jnp.max(s, axis=1, keepdims=True)
        p = jnp.exp(s - peak)
        total = jnp.sum(p, axis=1, keepdims=True)
        pb = p.astype(bf16)
        out = [
            matmul(pb[h * LAT : (h + 1) * LAT], lv[:, h * RHD : (h + 1) * RHD])
            for h in range(heads)
        ]
        lat_out_ref[...] = finish(out, peak, total, heads)

    x = patches_ref[...]
    kb = matmul(x, wk_ref[...]).astype(bf16)
    vb = matmul(x, wv_ref[...]).astype(bf16)
    here = pl.ds(pl.multiple_of(step * block, block), block)
    scores[:, here] = matmul_nt(qbd[...], kb) * scale
    for h in range(heads):
        values[h, here, :] = vb[:, h * RHD : (h + 1) * RHD]

    @pl.when(step == pl.num_programs(0) - 1)
    def _():
        clip = clip_ref[...]
        few = clips <= 8

        def find_peak(c, selected):
            s = scores[...]
            inside = clip == c
            peak = jnp.max(jnp.where(inside, s, masked_score), axis=1, keepdims=True)
            peaks[c] = peak
            return jnp.where(inside, peak, selected)

        selected = lax.fori_loop(
            0, clips, find_peak, jnp.zeros(scores.shape, f32), unroll=few
        )
        p = jnp.exp(scores[...] - selected)
        scores[...] = p
        pb = p.astype(bf16)
        group = masked.shape[1] // LAT

        def one_group(base, carry):
            totals = []
            for k in range(group):
                c = base * group + k
                inside = clip == c
                totals.append(
                    jnp.sum(jnp.where(inside, scores[...], 0.0), axis=1, keepdims=True)
                )
                keep = jnp.where(inside, 1.0, 0.0).astype(bf16)
                pc = scores[...].astype(bf16) * keep
                for h in range(heads):
                    masked[h, k * LAT : (k + 1) * LAT, :] = pc[h * LAT : (h + 1) * LAT]
            outs = [matmul(masked[h], values[h]) for h in range(heads)]
            for k in range(group):
                c = base * group + k
                out = [o[k * LAT : (k + 1) * LAT] for o in outs]
                out_ref[owner_ref[c]] = finish(out, peaks[c], totals[k], heads).astype(bf16)
            return carry

        lax.fori_loop(0, clips // group, one_group, 0, unroll=few)


def merge_kernel(got_ref, lat_ref, out_ref):
    groups = got_ref.shape[0]
    heads = 4
    width = heads * RHD

    def stats(tail):
        return sum(tail[:, i * heads : (i + 1) * heads] for i in range(3))

    def spread(w):
        lane = lax.broadcasted_iota(jnp.int32, (LAT, width), 1)
        full = jnp.broadcast_to(w[:, 0:1], (LAT, width))
        for h in range(1, heads):
            full = jnp.where(lane >= h * RHD, w[:, h : h + 1], full)
        return full

    lat_lse = stats(lat_ref[:, width : width + 3 * heads])
    lse = [
        stats(got_ref[g, :, width : width + 3 * heads].astype(f32)) for g in range(groups)
    ]
    best = functools.reduce(jnp.maximum, lse, lat_lse)
    weights = [jnp.exp(x - best) for x in lse]
    lat_weight = jnp.exp(lat_lse - best)
    total = sum(weights, lat_weight)
    mixed = spread(lat_weight / total) * lat_ref[:, :width]
    for g in range(groups):
        mixed = mixed + spread(weights[g] / total) * got_ref[g, :, :width].astype(f32)
    half = LAT // 2
    third = jnp.concatenate([mixed[:half, 256:320], mixed[half:, 256:320]], axis=1)
    packed = jnp.concatenate([mixed[:, :128], mixed[:, 128:256], third], axis=0).astype(bf16)
    for g in range(groups):
        out_ref[g] = packed


def cross_kernel(*refs, blocks, ways):
    mix = refs[:ways]
    w_out_ref, init_ref, cited_ref, q_ref, wk_ref, wv_ref = refs[ways : ways + 6]
    lat_ref, ctx_ref = refs[ways + 6 : ways + 8]
    latents, mixed, bias = refs[ways + 8 : ways + 11]
    kb, hp = pl.program_id(0), pl.program_id(1)
    clips = KEYS // LAT
    half = LAT // 2

    @pl.when(hp == 0)
    def _():
        tails = []
        for k in range(ways):
            for g in range(clips):
                rows = slice(g * LAT, (g + 1) * LAT)
                mixed[rows, k * 256 : k * 256 + 128] = mix[k][g, 0:64]
                mixed[rows, k * 256 + 128 : (k + 1) * 256] = mix[k][g, 64:128]
                low = slice(g * LAT, g * LAT + half)
                high = slice(g * LAT + half, (g + 1) * LAT)
                at = slice(ways * 256 + k * 64, ways * 256 + (k + 1) * 64)
                mixed[low, at] = mix[k][g, 128:160, 0:64]
                mixed[high, at] = mix[k][g, 128:160, 64:128]
        init = init_ref[...].astype(f32)
        lat = matmul(mixed[...], w_out_ref[...])
        for g in range(clips):
            rows = slice(g * LAT, (g + 1) * LAT)
            latents[rows] = (lat[rows] + init).astype(bf16)
        lat_ref[...] = latents[...]
        flags = cited_ref.shape[1]
        row = lax.broadcasted_iota(jnp.int32, (flags, KEYS), 0)
        col = lax.broadcasted_iota(jnp.int32, (flags, KEYS), 1)
        first = (row - kb * clips) * LAT
        expand = jnp.where((col >= first) & (col < first + LAT), 1.0, 0.0).astype(bf16)
        bias[...] = (matmul(cited_ref[...], expand) - 1.0) * -masked_score

    key = matmul(latents[...], wk_ref[...]).astype(bf16)
    value = matmul(latents[...], wv_ref[...]).astype(bf16)
    inv = 1.0 / math.sqrt(HD)
    for h in range(2):
        cols = slice(h * HD, (h + 1) * HD)
        s = matmul_nt(q_ref[:, cols], key[:, cols]) * inv + bias[...]
        if blocks == 1:
            top = jnp.max(s, axis=1, keepdims=True)
            p = jnp.exp(s - top)
            total = jnp.sum(p, axis=1, keepdims=True)
            o = matmul(p.astype(bf16), value[:, cols])
            ctx_ref[:, cols] = (o / total).astype(bf16)
        else:
            acc, tops, totals = refs[ways + 11 :]
            at = hp * 2 + h
            first = kb == 0
            old_top = jnp.where(first, masked_score, tops[at])
            top = jnp.maximum(old_top, jnp.max(s, axis=1, keepdims=True))
            alpha = jnp.where(first, 0.0, jnp.exp(old_top - top))
            p = jnp.where(s > 0.5 * masked_score, jnp.exp(s - top), 0.0)
            total = alpha * jnp.where(first, 0.0, totals[at]) + jnp.sum(p, axis=1, keepdims=True)
            o = alpha * jnp.where(first, 0.0, acc[at])
            o = o + matmul(p.astype(bf16), value[:, cols])
            tops[at] = top
            totals[at] = total
            acc[at] = o

            @pl.when(kb == blocks - 1)
            def _():
                ctx_ref[:, cols] = (o / total).astype(bf16)


def exchange(x, ways):
    out = [x]
    for k in range(1, ways):
        low = k & -k
        top = 1 << (k.bit_length() - 1)
        source = out[k ^ low] if k != low else x
        del top
        out.append(lax.ppermute(source, "mp", [(i, i ^ low) for i in range(ways)]))
    return out


def body(
    patches,
    clip_of,
    owner_of,
    cites,
    latent_init,
    w_query,
    w_key,
    w_value,
    w_out,
    wx_key,
    wx_value,
    queries,
):
    groups = lax.axis_size("seq")
    ways = lax.axis_size("mp")
    clip_total = owner_of.shape[0]
    rows, wide = patches.shape
    width = w_query.shape[1]
    heads = width // RHD
    block = 256

    w_parts = exchange(w_out, ways)
    w_cat = jnp.concatenate([w[:256] for w in w_parts] + [w[256:] for w in w_parts], axis=0)

    whole = lambda shape: pl.BlockSpec(shape, lambda *_: (0,) * len(shape))
    chunk = min(8, clip_total)
    packed, lat_part = pl.pallas_call(
        partial_kernel,
        grid_spec=pltpu.PrefetchScalarGridSpec(
            num_scalar_prefetch=1,
            grid=(rows // block,),
            in_specs=[
                whole((1, rows)),
                pl.BlockSpec((block, wide), lambda i, *_: (i, 0)),
                whole((LAT, wide)),
                whole((wide, width)),
                whole((wide, width)),
                whole((wide, width)),
            ],
            out_specs=[whole((groups, LAT, 384)), whole((LAT, 384))],
            scratch_shapes=[
                pltpu.VMEM((heads * LAT, width), bf16),
                pltpu.VMEM((heads * LAT, rows), f32),
                pltpu.VMEM((heads, rows, RHD), bf16),
                pltpu.VMEM((heads, chunk * LAT, rows), bf16),
                pltpu.VMEM((clip_total, heads * LAT, 1), f32),
            ],
        ),
        out_shape=[
            jax.ShapeDtypeStruct((groups, LAT, 384), bf16),
            jax.ShapeDtypeStruct((LAT, 384), f32),
        ],
        name="partials",
    )(owner_of, clip_of.reshape(1, rows), patches, latent_init, w_query, w_key, w_value)

    got = lax.all_to_all(packed, "seq", split_axis=0, concat_axis=0, tiled=True)

    spread = pl.pallas_call(
        merge_kernel,
        out_shape=jax.ShapeDtypeStruct((groups, 160, 128), bf16),
        name="merge",
    )(got, lat_part)

    everyone = lax.all_to_all(spread, "seq", split_axis=0, concat_axis=0, tiled=True)
    mixes = exchange(everyone, ways)

    question_count = cites.shape[0]
    question_len = queries.shape[0] // question_count
    cite_hot = cites[:, :, None] == jnp.arange(clip_total, dtype=jnp.int32)[None, None, :]
    cite_owner = jnp.sum(cite_hot * owner_of[None, None, :], axis=2)
    flags = -(-groups // 128) * 128
    cited = jnp.any(
        cite_owner[:, :, None] == jnp.arange(flags, dtype=jnp.int32)[None, None, :], axis=1
    )
    token_cited = jnp.repeat(cited.astype(bf16), question_len, axis=0)

    tokens, cross = queries.shape
    blocks = groups * LAT // KEYS
    pair = 2 * HD
    per_pair = lambda shape: pl.BlockSpec(shape, lambda kb, hp: (0, hp))
    scratch = [
        pltpu.VMEM((KEYS, wide), bf16),
        pltpu.VMEM((KEYS, wide), bf16),
        pltpu.VMEM((tokens, KEYS), f32),
    ]
    if blocks > 1:
        scratch += [
            pltpu.VMEM((cross // HD, tokens, HD), f32),
            pltpu.VMEM((cross // HD, tokens, 1), f32),
            pltpu.VMEM((cross // HD, tokens, 1), f32),
        ]
    latents, context = pl.pallas_call(
        functools.partial(cross_kernel, blocks=blocks, ways=ways),
        grid=(blocks, cross // pair),
        in_specs=[pl.BlockSpec((KEYS // LAT, 160, 128), lambda kb, hp: (kb, 0, 0))] * ways
        + [
            whole((wide, wide)),
            whole((LAT, wide)),
            whole((tokens, flags)),
            per_pair((tokens, pair)),
            per_pair((wide, pair)),
            per_pair((wide, pair)),
        ],
        out_specs=[
            pl.BlockSpec((KEYS, wide), lambda kb, hp: (kb, 0)),
            per_pair((tokens, pair)),
        ],
        out_shape=[
            jax.ShapeDtypeStruct((groups * LAT, wide), bf16),
            jax.ShapeDtypeStruct((tokens, cross), bf16),
        ],
        scratch_shapes=scratch,
        name="cross",
    )(*mixes, w_cat, latent_init, token_cited, queries, wx_key, wx_value)
    resampled = lax.dynamic_slice_in_dim(latents, lax.axis_index("seq") * LAT, LAT, axis=0)
    return (resampled, context)


def solution(mesh):
    in_specs = (
        P("seq", None),
        P("seq", None),
        P(),
        P("seq", None),
        P(),
        P(None, "mp"),
        P(None, "mp"),
        P(None, "mp"),
        P("mp", None),
        P(None, "mp"),
        P(None, "mp"),
        P("seq", "mp"),
    )
    out_specs = (P("seq", None), P("seq", "mp"))
    return jax.shard_map(body, mesh=mesh, in_specs=in_specs, out_specs=out_specs, check_vma=False)
```

```python
import functools
import math

import jax
import jax.numpy as jnp
from jax import lax
from jax.experimental import pallas as pl
from jax.experimental.pallas import tpu as pltpu
from jax.sharding import PartitionSpec as P

RHD = 80
LAT = 64
HD = 128
KEYS = 512

masked_score = -1e30
f32 = jnp.float32
bf16 = jnp.bfloat16


def matmul(a, b):
    return jnp.dot(a, b, preferred_element_type=f32)


def matmul_nt(a, b):
    return lax.dot_general(a, b, (((1,), (1,)), ((), ())), preferred_element_type=f32)


def split3(x):
    a = x.astype(bf16).astype(f32)
    b = (x - a).astype(bf16).astype(f32)
    return a, b, x - a - b


def pack(cols):
    x = jnp.concatenate(cols, axis=1)
    half = LAT // 2
    third = jnp.concatenate([x[:half, 256:320], x[half:, 256:320]], axis=1)
    return jnp.concatenate([x[:, :128], x[:, 128:256], third], axis=0)


def partial_kernel(
    owner_ref, clip_ref, patches_ref, lat_ref, wq_ref, wk_ref, wv_ref,
    out_ref, lat_out_ref, qbd, scores, values, masked, peaks, totals, lses,
):
    step = pl.program_id(0)
    block = patches_ref.shape[0]
    width = wq_ref.shape[0]
    heads = width // RHD
    clips = owner_ref.shape[0]
    scale = 1.0 / math.sqrt(RHD)

    @pl.when(step == 0)
    def _():
        lat = lat_ref[...]
        q = matmul_nt(lat, wq_ref[...])
        lane = lax.broadcasted_iota(jnp.int32, q.shape, 1)
        for h in range(heads):
            inside = (lane >= h * RHD) & (lane < (h + 1) * RHD)
            qbd[h * LAT : (h + 1) * LAT, :] = jnp.where(inside, q, 0.0).astype(bf16)
        lk = matmul_nt(wk_ref[...], lat).astype(bf16)
        lv = matmul_nt(wv_ref[...], lat).astype(bf16)
        s = matmul(qbd[...], lk) * scale
        peak = jnp.max(s, axis=1, keepdims=True)
        p = jnp.exp(s - peak)
        total = jnp.sum(p, axis=1, keepdims=True)
        pb = p.astype(bf16)
        inv = 1.0 / total
        out = []
        for h in range(heads):
            rows = slice(h * LAT, (h + 1) * LAT)
            out.append(matmul_nt(pb[rows], lv[h * RHD : (h + 1) * RHD]) * inv[rows])
        lat_out_ref[0:160] = pack(out)
        lse = jnp.broadcast_to(peak + jnp.log(total), (heads * LAT, 128)).T[0:8]
        for i in range(heads * LAT // 128):
            lat_out_ref[160 + i : 161 + i] = lse[0:1, i * 128 : (i + 1) * 128]

    x = patches_ref[...]
    here = pl.ds(pl.multiple_of(step * block, block), block)
    kt = matmul_nt(wk_ref[...], x).astype(bf16)
    values[:, here] = matmul_nt(wv_ref[...], x).astype(bf16)
    scores[:, here] = matmul(qbd[...], kt) * scale

    @pl.when(step == pl.num_programs(0) - 1)
    def _():
        clip = clip_ref[...]
        group = masked.shape[1] // LAT
        rounds = clips // group
        tall = 16
        lane = lax.broadcasted_iota(jnp.int32, (tall, 128), 1)

        def peak_pass(rows):
            s = scores[rows, :]

            def one(base, carry):
                selected, stat = carry
                for k in range(group):
                    c = base * group + k
                    inside = clip == c
                    peak = jnp.max(jnp.where(inside, s, masked_score), axis=1, keepdims=True)
                    selected = jnp.where(inside, peak, selected)
                    stat = jnp.where(lane == c, peak, stat)
                return selected, stat

            init = (jnp.zeros(s.shape, f32), jnp.zeros((tall, 128), f32))
            if rounds == 1:
                selected, stat = one(0, init)
            else:
                selected, stat = lax.fori_loop(0, rounds, one, init)
            peaks[rows, :] = stat
            return jnp.exp(s - selected)

        def mask_pass(h, r, p, base, stat):
            pb = p.astype(bf16)
            for k in range(group):
                c = base * group + k
                inside = clip == c
                total = jnp.sum(jnp.where(inside, p, 0.0), axis=1, keepdims=True)
                stat = jnp.where(lane == c, total, stat)
                keep = jnp.where(inside, 1.0, 0.0).astype(bf16)
                masked[h, k * LAT + r * tall : k * LAT + (r + 1) * tall, :] = pb * keep
            return stat

        def rows_of(h, r):
            return slice(h * LAT + r * tall, h * LAT + (r + 1) * tall)

        def emit(base, outs):
            for k in range(group):
                c = base * group + k
                cols = []
                for h in range(heads):
                    t = totals[h * LAT : (h + 1) * LAT, :]
                    pick = lax.broadcasted_iota(jnp.int32, t.shape, 1) == c
                    t = jnp.sum(jnp.where(pick, t, 0.0), axis=1, keepdims=True)
                    inv = 1.0 / jnp.where(t > 0, t, 1.0)
                    cols.append(outs[h][k * LAT : (k + 1) * LAT] * inv)
                out_ref[owner_ref[c], 0:160, :] = pack(cols).astype(bf16)

        if rounds == 1:
            outs = []
            for h in range(heads):
                for r in range(LAT // tall):
                    rows = rows_of(h, r)
                    p = peak_pass(rows)
                    totals[rows, :] = mask_pass(h, r, p, 0, jnp.zeros((tall, 128), f32))
                outs.append(matmul_nt(masked[h], values[h * RHD : (h + 1) * RHD, :]))
            emit(0, outs)
        else:
            totals[...] = jnp.zeros(totals.shape, f32)
            for h in range(heads):
                for r in range(LAT // tall):
                    rows = rows_of(h, r)
                    scores[rows, :] = peak_pass(rows)

            def one_round(base, carry):
                outs = []
                for h in range(heads):
                    for r in range(LAT // tall):
                        rows = rows_of(h, r)
                        totals[rows, :] = mask_pass(h, r, scores[rows, :], base, totals[rows, :])
                    outs.append(matmul_nt(masked[h], values[h * RHD : (h + 1) * RHD, :]))
                emit(base, outs)
                return carry

            lax.fori_loop(0, rounds, one_round, 0)

        t = totals[...]
        live = t > 0
        lse = jnp.where(live, peaks[...] + jnp.log(jnp.where(live, t, 1.0)), masked_score)
        for i, part in enumerate(split3(lse.T)):
            lses[i] = part

        def tail(c, carry):
            rows = []
            for i in range(3):
                row = lses[i, pl.ds(c, 1), :]
                rows += [row[:, j * 128 : (j + 1) * 128] for j in range(heads * LAT // 128)]
            rows.append(jnp.zeros((16 - len(rows), 128), f32))
            out_ref[owner_ref[c], 160:176, :] = jnp.concatenate(rows, axis=0).astype(bf16)
            return carry

        if clips <= 8:
            for c in range(clips):
                tail(c, 0)
        else:
            lax.fori_loop(0, clips, tail, 0)


def merge_kernel(got_ref, lat_ref, out_ref):
    groups = got_ref.shape[0]
    lse = [lat_ref[160:162]]
    for g in range(groups):
        tail = got_ref[g, 160:176, :].astype(f32)
        lse.append(tail[0:2] + tail[2:4] + tail[4:6])
    best = functools.reduce(jnp.maximum, lse)
    weights = [jnp.exp(x - best) for x in lse]
    inv = 1.0 / sum(weights[1:], weights[0])
    rows = [w * inv for w in weights]
    short = -2 * len(rows) % 128
    table = jnp.concatenate(rows + [jnp.zeros((short, 128), f32)], axis=0).T
    lane = lax.broadcasted_iota(jnp.int32, (LAT, 128), 1)
    half = LAT // 2
    total = [0.0, 0.0, 0.0]
    for g in range(groups + 1):
        col = [
            table[(h % 2) * LAT : (h % 2 + 1) * LAT, 2 * g + h // 2 : 2 * g + h // 2 + 1]
            for h in range(4)
        ]
        factors = (
            jnp.where(lane < 80, col[0], col[1]),
            jnp.where(lane < 32, col[1], jnp.where(lane < 112, col[2], col[3])),
            jnp.where(lane[:half] < 64, col[3][:half], col[3][half:]),
        )
        for i, (lo, hi) in enumerate(((0, 64), (64, 128), (128, 160))):
            piece = lat_ref[lo:hi] if g == 0 else got_ref[g - 1, lo:hi, :].astype(f32)
            total[i] = total[i] + factors[i] * piece
    for i, (lo, hi) in enumerate(((0, 64), (64, 128), (128, 160))):
        piece = total[i].astype(bf16)
        for g in range(groups):
            out_ref[g, lo:hi, :] = piece


def cross_kernel(me_ref, *refs, blocks, ways):
    mix = refs[:ways]
    w_refs = refs[ways : 2 * ways]
    init_ref, cited_ref, q_ref, wk_ref, wv_ref = refs[2 * ways : 2 * ways + 5]
    lat_ref, ctx_ref = refs[2 * ways + 5 : 2 * ways + 7]
    latents, mixed, bias, w_all, sems = refs[2 * ways + 7 : 2 * ways + 12]
    kb, hp = pl.program_id(0), pl.program_id(1)
    clips = KEYS // LAT
    half = LAT // 2
    tokens = q_ref.shape[0]
    questions = cited_ref.shape[0]

    def copies():
        for k in range(ways):
            yield pltpu.make_async_copy(
                w_refs[k].at[0:256], w_all.at[k * 256 : (k + 1) * 256], sems.at[2 * k]
            )
            at = ways * 256 + k * 64
            yield pltpu.make_async_copy(
                w_refs[k].at[256:320], w_all.at[at : at + 64], sems.at[2 * k + 1]
            )

    @pl.when(hp == 0)
    def _():
        @pl.when(kb == 0)
        def _():
            for copy in copies():
                copy.start()

        for k in range(ways):
            for g in range(clips):
                rows = slice(g * LAT, (g + 1) * LAT)
                mixed[rows, k * 256 : k * 256 + 128] = mix[k][g, 0:64]
                mixed[rows, k * 256 + 128 : (k + 1) * 256] = mix[k][g, 64:128]
                low = slice(g * LAT, g * LAT + half)
                high = slice(g * LAT + half, (g + 1) * LAT)
                at = slice(ways * 256 + k * 64, ways * 256 + (k + 1) * 64)
                mixed[low, at] = mix[k][g, 128:160, 0:64]
                mixed[high, at] = mix[k][g, 128:160, 64:128]
        flags = cited_ref.shape[1]
        row = lax.broadcasted_iota(jnp.int32, (flags, KEYS), 0)
        col = lax.broadcasted_iota(jnp.int32, (flags, KEYS), 1)
        first = (row - kb * clips) * LAT
        expand = jnp.where((col >= first) & (col < first + LAT), 1.0, 0.0).astype(bf16)
        asked = matmul(cited_ref[...], expand).astype(bf16)
        row = lax.broadcasted_iota(jnp.int32, (tokens, questions), 0)
        first = lax.broadcasted_iota(jnp.int32, (tokens, questions), 1) * (tokens // questions)
        repeat = (row >= first) & (row < first + tokens // questions)
        repeat = jnp.where(repeat, 1.0, 0.0).astype(bf16)
        bias[...] = (matmul(repeat, asked) - 1.0) * -masked_score

        @pl.when(kb == 0)
        def _():
            for copy in copies():
                copy.wait()

        init = init_ref[...].astype(f32)
        lat = matmul(mixed[...], w_all[...])
        for g in range(clips):
            rows = slice(g * LAT, (g + 1) * LAT)
            latents[rows] = (lat[rows] + init).astype(bf16)
        me = me_ref[0]

        @pl.when(me // clips == kb)
        def _():
            lat_ref[...] = latents[pl.ds(pl.multiple_of(me % clips * LAT, LAT), LAT), :]

    key = matmul(latents[...], wk_ref[...]).astype(bf16)
    value = matmul(latents[...], wv_ref[...]).astype(bf16)
    inv = 1.0 / math.sqrt(HD)
    tall = min(128, tokens)
    for h in range(2):
        cols = slice(h * HD, (h + 1) * HD)
        for r in range(tokens // tall):
            rows = slice(r * tall, (r + 1) * tall)
            s = matmul_nt(q_ref[rows, cols], key[:, cols]) * inv + bias[rows]
            if blocks == 1:
                top = jnp.max(s, axis=1, keepdims=True)
                p = jnp.exp(s - top)
                total = jnp.sum(p, axis=1, keepdims=True)
                o = matmul(p.astype(bf16), value[:, cols])
                ctx_ref[rows, cols] = (o * (1.0 / total)).astype(bf16)
            else:
                acc, tops, totals = refs[2 * ways + 12 :]
                at = hp * 2 + h
                first = kb == 0
                old_top = jnp.where(first, masked_score, tops[at, rows])
                top = jnp.maximum(old_top, jnp.max(s, axis=1, keepdims=True))
                alpha = jnp.where(first, 0.0, jnp.exp(old_top - top))
                p = jnp.where(s > 0.5 * masked_score, jnp.exp(s - top), 0.0)
                total = jnp.where(first, 0.0, totals[at, rows]) * alpha
                total = total + jnp.sum(p, axis=1, keepdims=True)
                o = jnp.where(first, 0.0, acc[at, rows]) * alpha
                o = o + matmul(p.astype(bf16), value[:, cols])
                tops[at, rows] = top
                totals[at, rows] = total
                acc[at, rows] = o
                ctx_ref[rows, cols] = (o * (1.0 / jnp.maximum(total, 1e-30))).astype(bf16)


def exchange(x, ways):
    out = [x]
    for k in range(1, ways):
        low = k & -k
        source = out[k ^ low] if k != low else x
        out.append(lax.ppermute(source, "mp", [(i, i ^ low) for i in range(ways)]))
    return out


def body(
    patches,
    clip_of,
    owner_of,
    cites,
    latent_init,
    w_query,
    w_key,
    w_value,
    w_out,
    wx_key,
    wx_value,
    queries,
):
    groups = lax.axis_size("seq")
    ways = lax.axis_size("mp")
    clip_total = owner_of.shape[0]
    rows, wide = patches.shape
    width = w_query.shape[1]
    heads = width // RHD
    block = 256

    w_parts = exchange(w_out, ways)

    whole = lambda shape: pl.BlockSpec(shape, lambda *_: (0,) * len(shape))
    chunk = min(8, clip_total)
    packed, lat_part = pl.pallas_call(
        partial_kernel,
        grid_spec=pltpu.PrefetchScalarGridSpec(
            num_scalar_prefetch=1,
            grid=(rows // block,),
            in_specs=[
                whole((1, rows)),
                pl.BlockSpec((block, wide), lambda i, *_: (i, 0)),
                whole((LAT, wide)),
                whole((width, wide)),
                whole((width, wide)),
                whole((width, wide)),
            ],
            out_specs=[whole((groups, 176, 128)), whole((168, 128))],
            scratch_shapes=[
                pltpu.VMEM((heads * LAT, width), bf16),
                pltpu.VMEM((heads * LAT, rows), f32),
                pltpu.VMEM((width, rows), bf16),
                pltpu.VMEM((heads, chunk * LAT, rows), bf16),
                pltpu.VMEM((heads * LAT, 128), f32),
                pltpu.VMEM((heads * LAT, 128), f32),
                pltpu.VMEM((3, 128, heads * LAT), f32),
            ],
        ),
        out_shape=[
            jax.ShapeDtypeStruct((groups, 176, 128), bf16),
            jax.ShapeDtypeStruct((168, 128), f32),
        ],
        name="partials",
    )(owner_of, clip_of.reshape(1, rows), patches, latent_init, w_query.T, w_key.T, w_value.T)

    got = lax.all_to_all(packed, "seq", split_axis=0, concat_axis=0, tiled=True)

    spread = pl.pallas_call(
        merge_kernel,
        out_shape=jax.ShapeDtypeStruct((groups, 160, 128), bf16),
        name="merge",
    )(got, lat_part)

    everyone = lax.all_to_all(spread, "seq", split_axis=0, concat_axis=0, tiled=True)
    mixes = exchange(everyone, ways)

    cite_hot = cites[:, :, None] == jnp.arange(clip_total, dtype=jnp.int32)[None, None, :]
    cite_owner = jnp.sum(cite_hot * owner_of[None, None, :], axis=2)
    flags = -(-groups // 128) * 128
    cited = jnp.any(
        cite_owner[:, :, None] == jnp.arange(flags, dtype=jnp.int32)[None, None, :], axis=1
    ).astype(bf16)

    tokens, cross = queries.shape
    blocks = groups * LAT // KEYS
    pair = 2 * HD
    per_pair = lambda shape: pl.BlockSpec(shape, lambda kb, hp, *_: (0, hp))
    anywhere = pl.BlockSpec(memory_space=pl.ANY)
    scratch = [
        pltpu.VMEM((KEYS, wide), bf16),
        pltpu.VMEM((KEYS, wide), bf16),
        pltpu.VMEM((tokens, KEYS), f32),
        pltpu.VMEM((wide, wide), bf16),
        pltpu.SemaphoreType.DMA((2 * ways,)),
    ]
    if blocks > 1:
        scratch += [
            pltpu.VMEM((cross // HD, tokens, HD), f32),
            pltpu.VMEM((cross // HD, tokens, 1), f32),
            pltpu.VMEM((cross // HD, tokens, 1), f32),
        ]
    resampled, context = pl.pallas_call(
        functools.partial(cross_kernel, blocks=blocks, ways=ways),
        grid_spec=pltpu.PrefetchScalarGridSpec(
            num_scalar_prefetch=1,
            grid=(blocks, cross // pair),
            in_specs=[pl.BlockSpec((KEYS // LAT, 160, 128), lambda kb, hp, *_: (kb, 0, 0))] * ways
            + [anywhere] * ways
            + [
                whole((LAT, wide)),
                whole(cited.shape),
                per_pair((tokens, pair)),
                per_pair((wide, pair)),
                per_pair((wide, pair)),
            ],
            out_specs=[whole((LAT, wide)), per_pair((tokens, pair))],
            scratch_shapes=scratch,
        ),
        out_shape=[
            jax.ShapeDtypeStruct((LAT, wide), bf16),
            jax.ShapeDtypeStruct((tokens, cross), bf16),
        ],
        name="cross",
    )(
        lax.axis_index("seq").astype(jnp.int32).reshape(1),
        *mixes,
        *w_parts,
        latent_init,
        cited,
        queries,
        wx_key,
        wx_value,
    )
    return (resampled, context)


def solution(mesh):
    in_specs = (
        P("seq", None),
        P("seq", None),
        P(),
        P("seq", None),
        P(),
        P(None, "mp"),
        P(None, "mp"),
        P(None, "mp"),
        P("mp", None),
        P(None, "mp"),
        P(None, "mp"),
        P("seq", "mp"),
    )
    out_specs = (P("seq", None), P("seq", "mp"))
    return jax.shard_map(body, mesh=mesh, in_specs=in_specs, out_specs=out_specs, check_vma=False)
```

```python
import functools
import math

import jax
import jax.numpy as jnp
from jax import lax
from jax.experimental import pallas as pl
from jax.experimental.pallas import tpu as pltpu
from jax.sharding import PartitionSpec as P

RHD = 80
LAT = 64
HD = 128
KEYS = 512

masked_score = -1e30
f32 = jnp.float32
bf16 = jnp.bfloat16


def matmul(a, b):
    return jnp.dot(a, b, preferred_element_type=f32)


def matmul_nt(a, b):
    return lax.dot_general(a, b, (((1,), (1,)), ((), ())), preferred_element_type=f32)


def split3(x):
    a = x.astype(bf16).astype(f32)
    b = (x - a).astype(bf16).astype(f32)
    return a, b, x - a - b


def pack(cols):
    x = jnp.concatenate(cols, axis=1)
    half = LAT // 2
    third = jnp.concatenate([x[:half, 256:320], x[half:, 256:320]], axis=1)
    return jnp.concatenate([x[:, :128], x[:, 128:256], third], axis=0)


def head_mask(q):
    lane = lax.broadcasted_iota(jnp.int32, q.shape, 1)
    heads = q.shape[1] // RHD
    return [
        jnp.where((lane >= h * RHD) & (lane < (h + 1) * RHD), q, 0.0).astype(bf16)
        for h in range(heads)
    ]


def partial_kernel(
    owner_ref, clip_ref, lat_ref, patches_hbm, wq_hbm, wk_hbm, wv_hbm,
    out_ref, query_ref, patches, wq_ref, wk_ref, wv_ref, sems,
    scores, values, masked, peaks, totals, lses,
):
    pieces = sems.shape[0] - 3
    block = patches.shape[0] // pieces
    width = wq_ref.shape[0]
    heads = width // RHD
    clips = owner_ref.shape[0]
    scale = 1.0 / math.sqrt(RHD)

    def patch_copy(i):
        rows = slice(i * block, (i + 1) * block)
        return pltpu.make_async_copy(patches_hbm.at[rows], patches.at[rows], sems.at[3 + i])

    fetch_q = pltpu.make_async_copy(wq_hbm, wq_ref, sems.at[0])
    fetch_k = pltpu.make_async_copy(wk_hbm, wk_ref, sems.at[1])
    fetch_v = pltpu.make_async_copy(wv_hbm, wv_ref, sems.at[2])
    fetch_q.start()
    fetch_k.start()
    patch_copy(0).start()
    fetch_v.start()
    for i in range(1, pieces):
        patch_copy(i).start()
    fetch_q.wait()
    for h, rows in enumerate(head_mask(matmul_nt(lat_ref[...], wq_ref[...]))):
        query_ref[h * LAT : (h + 1) * LAT, :] = rows
    fetch_k.wait()
    for i in range(pieces):
        here = slice(i * block, (i + 1) * block)
        patch_copy(i).wait()
        x = patches[here, :]
        kt = matmul_nt(wk_ref[...], x).astype(bf16)
        scores[:, here] = matmul(query_ref[...], kt) * scale
        if i == 0:
            fetch_v.wait()
        values[:, here] = matmul_nt(wv_ref[...], x).astype(bf16)

    clip = clip_ref[...]
    group = masked.shape[1] // LAT
    rounds = clips // group
    tall = 16
    lane = lax.broadcasted_iota(jnp.int32, (tall, 128), 1)

    def peak_pass(rows):
        s = scores[rows, :]

        def one(base, carry):
            selected, stat = carry
            for k in range(group):
                c = base * group + k
                inside = clip == c
                peak = jnp.max(jnp.where(inside, s, masked_score), axis=1, keepdims=True)
                selected = jnp.where(inside, peak, selected)
                stat = jnp.where(lane == c, peak, stat)
            return selected, stat

        init = (jnp.zeros(s.shape, f32), jnp.zeros((tall, 128), f32))
        if rounds == 1:
            selected, stat = one(0, init)
        else:
            selected, stat = lax.fori_loop(0, rounds, one, init)
        peaks[rows, :] = stat
        return jnp.exp(s - selected)

    def mask_pass(h, r, p, base, stat):
        pb = p.astype(bf16)
        for k in range(group):
            c = base * group + k
            inside = clip == c
            total = jnp.sum(jnp.where(inside, p, 0.0), axis=1, keepdims=True)
            stat = jnp.where(lane == c, total, stat)
            keep = jnp.where(inside, 1.0, 0.0).astype(bf16)
            masked[h, k * LAT + r * tall : k * LAT + (r + 1) * tall, :] = pb * keep
        return stat

    def rows_of(h, r):
        return slice(h * LAT + r * tall, h * LAT + (r + 1) * tall)

    def emit(base, outs):
        for k in range(group):
            c = base * group + k
            cols = []
            for h in range(heads):
                t = totals[h * LAT : (h + 1) * LAT, :]
                pick = lax.broadcasted_iota(jnp.int32, t.shape, 1) == c
                t = jnp.sum(jnp.where(pick, t, 0.0), axis=1, keepdims=True)
                inv = 1.0 / jnp.where(t > 0, t, 1.0)
                cols.append(outs[h][k * LAT : (k + 1) * LAT] * inv)
            out_ref[owner_ref[c], 0:160, :] = pack(cols).astype(bf16)

    if rounds == 1:
        outs = []
        for h in range(heads):
            for r in range(LAT // tall):
                rows = rows_of(h, r)
                p = peak_pass(rows)
                totals[rows, :] = mask_pass(h, r, p, 0, jnp.zeros((tall, 128), f32))
            outs.append(matmul_nt(masked[h], values[h * RHD : (h + 1) * RHD, :]))
        emit(0, outs)
    else:
        totals[...] = jnp.zeros(totals.shape, f32)
        for h in range(heads):
            for r in range(LAT // tall):
                rows = rows_of(h, r)
                scores[rows, :] = peak_pass(rows)

        def one_round(base, carry):
            outs = []
            for h in range(heads):
                for r in range(LAT // tall):
                    rows = rows_of(h, r)
                    totals[rows, :] = mask_pass(h, r, scores[rows, :], base, totals[rows, :])
                outs.append(matmul_nt(masked[h], values[h * RHD : (h + 1) * RHD, :]))
            emit(base, outs)
            return carry

        lax.fori_loop(0, rounds, one_round, 0)

    t = totals[...]
    live = t > 0
    lse = jnp.where(live, peaks[...] + jnp.log(jnp.where(live, t, 1.0)), masked_score)
    for i, part in enumerate(split3(lse.T)):
        lses[i] = part

    def tail(c, carry):
        rows = []
        for i in range(3):
            row = lses[i, pl.ds(c, 1), :]
            rows += [row[:, j * 128 : (j + 1) * 128] for j in range(heads * LAT // 128)]
        rows.append(jnp.zeros((16 - len(rows), 128), f32))
        out_ref[owner_ref[c], 160:176, :] = jnp.concatenate(rows, axis=0).astype(bf16)
        return carry

    if clips <= 8:
        for c in range(clips):
            tail(c, 0)
    else:
        lax.fori_loop(0, clips, tail, 0)


def latent_kernel(lat_ref, query_ref, wk_ref, wv_ref, out_ref):
    heads = wk_ref.shape[0] // RHD
    lat = lat_ref[...]
    lk = matmul_nt(wk_ref[...], lat).astype(bf16)
    lv = matmul_nt(wv_ref[...], lat).astype(bf16)
    s = matmul(query_ref[...], lk) * (1.0 / math.sqrt(RHD))
    peak = jnp.max(s, axis=1, keepdims=True)
    p = jnp.exp(s - peak)
    total = jnp.sum(p, axis=1, keepdims=True)
    pb = p.astype(bf16)
    inv = 1.0 / total
    out = []
    for h in range(heads):
        rows = slice(h * LAT, (h + 1) * LAT)
        out.append(matmul_nt(pb[rows], lv[h * RHD : (h + 1) * RHD]) * inv[rows])
    out_ref[0:160] = pack(out)
    lse = jnp.broadcast_to(peak + jnp.log(total), (heads * LAT, 128)).T[0:8]
    for i in range(heads * LAT // 128):
        out_ref[160 + i : 161 + i] = lse[0:1, i * 128 : (i + 1) * 128]


def merge_kernel(got_ref, lat_ref, out_ref):
    groups = got_ref.shape[0]
    lse = [lat_ref[160:162]]
    for g in range(groups):
        tail = got_ref[g, 160:176, :].astype(f32)
        lse.append(tail[0:2] + tail[2:4] + tail[4:6])
    best = functools.reduce(jnp.maximum, lse)
    weights = [jnp.exp(x - best) for x in lse]
    inv = 1.0 / sum(weights[1:], weights[0])
    rows = [w * inv for w in weights]
    short = -2 * len(rows) % 128
    table = jnp.concatenate(rows + [jnp.zeros((short, 128), f32)], axis=0).T
    lane = lax.broadcasted_iota(jnp.int32, (LAT, 128), 1)
    half = LAT // 2
    total = [0.0, 0.0, 0.0]
    for g in range(groups + 1):
        col = [
            table[(h % 2) * LAT : (h % 2 + 1) * LAT, 2 * g + h // 2 : 2 * g + h // 2 + 1]
            for h in range(4)
        ]
        factors = (
            jnp.where(lane < 80, col[0], col[1]),
            jnp.where(lane < 32, col[1], jnp.where(lane < 112, col[2], col[3])),
            jnp.where(lane[:half] < 64, col[3][:half], col[3][half:]),
        )
        for i, (lo, hi) in enumerate(((0, 64), (64, 128), (128, 160))):
            piece = lat_ref[lo:hi] if g == 0 else got_ref[g - 1, lo:hi, :].astype(f32)
            total[i] = total[i] + factors[i] * piece
    for i, (lo, hi) in enumerate(((0, 64), (64, 128), (128, 160))):
        piece = total[i].astype(bf16)
        for g in range(groups):
            out_ref[g, lo:hi, :] = piece


def project(mixes, ways):
    clips = KEYS // LAT
    half = LAT // 2
    total = None
    for i in range(0, len(mixes), 2):
        folded = []
        for mix, w in zip(mixes[i : i + 2], ways[i : i + 2]):
            x = jnp.concatenate(
                [mix[:, 0:64].reshape(KEYS, 128), mix[:, 64:128].reshape(KEYS, 128)], axis=1
            )
            part = matmul(x, w[0:256])
            total = part if total is None else total + part
            folded.append(mix[:, 128:160])
        low = jnp.concatenate([t[:, :, 0:64] for t in folded], axis=2)
        high = jnp.concatenate([t[:, :, 64:128] for t in folded], axis=2)
        x = jnp.concatenate([low, high], axis=1).reshape(KEYS, 128)
        total = total + matmul(x, jnp.concatenate([w[256:320] for w in ways[i : i + 2]], axis=0))
    return total


def begin_kernel(a_ref, b_ref, wa_ref, wb_ref, init_ref, out_ref):
    init = init_ref[...].astype(f32)
    part = project([a_ref[...], b_ref[...]], [wa_ref[...], wb_ref[...]])
    for g in range(KEYS // LAT):
        rows = slice(g * LAT, (g + 1) * LAT)
        out_ref[rows] = part[rows] + init


def cross_kernel(me_ref, *refs, blocks, ways):
    mix = refs[:ways]
    w_refs = refs[ways : 2 * ways]
    init_ref, cited_ref, q_ref, wk_ref, wv_ref = refs[2 * ways : 2 * ways + 5]
    lat_ref, ctx_ref = refs[2 * ways + 5 : 2 * ways + 7]
    latents, bias, keys, vals, scores, weights = refs[2 * ways + 7 : 2 * ways + 13]
    clips = KEYS // LAT
    tokens = q_ref.shape[0]
    questions = cited_ref.shape[0]
    heads = q_ref.shape[1] // HD
    inv = 1.0 / math.sqrt(HD)
    tall = min(32, tokens)
    me = me_ref[0]

    def one_block(kb, carry):
        flags = cited_ref.shape[1]
        row = lax.broadcasted_iota(jnp.int32, (flags, KEYS), 0)
        col = lax.broadcasted_iota(jnp.int32, (flags, KEYS), 1)
        first = (row - kb * clips) * LAT
        expand = jnp.where((col >= first) & (col < first + LAT), 1.0, 0.0).astype(bf16)
        asked = matmul(cited_ref[...], expand).astype(bf16)
        row = lax.broadcasted_iota(jnp.int32, (tokens, questions), 0)
        first = lax.broadcasted_iota(jnp.int32, (tokens, questions), 1) * (tokens // questions)
        repeat = (row >= first) & (row < first + tokens // questions)
        repeat = jnp.where(repeat, 1.0, 0.0).astype(bf16)
        bias[...] = (matmul(repeat, asked) - 1.0) * -masked_score

        here = pl.ds(kb * clips, clips)
        part = project([m[here] for m in mix], [w[...] for w in w_refs])
        if init_ref.shape[0] == KEYS:
            latents[...] = (part + init_ref[...]).astype(bf16)
        else:
            init = init_ref[...].astype(f32)
            for g in range(clips):
                rows = slice(g * LAT, (g + 1) * LAT)
                latents[rows] = (part[rows] + init).astype(bf16)

        @pl.when(me // clips == kb)
        def _():
            lat_ref[...] = latents[pl.ds(pl.multiple_of(me % clips * LAT, LAT), LAT), :]

        for h in range(heads):
            cols = slice(h * HD, (h + 1) * HD)
            if h % 2 == 0:
                pair = slice(h * HD, (h + 2) * HD)
                keys[:, pair] = matmul(latents[...], wk_ref[:, pair]).astype(bf16)
                vals[:, pair] = matmul(latents[...], wv_ref[:, pair]).astype(bf16)
            slot = h % scores.shape[0]
            scores[slot] = matmul_nt(q_ref[:, cols], keys[:, cols])
            if blocks > 1:
                acc, tops, totals = refs[2 * ways + 13 :]
            sums = []
            for r in range(tokens // tall):
                rows = slice(r * tall, (r + 1) * tall)
                s = scores[slot, rows] * inv + bias[rows]
                top = jnp.max(s, axis=1, keepdims=True)
                if blocks > 1:
                    old = jnp.where(kb == 0, masked_score, tops[h, rows])
                    top = jnp.maximum(old, top)
                    tops[h, rows] = top
                    alpha = jnp.where(kb == 0, 0.0, jnp.exp(old - top))
                    p = jnp.where(s > 0.5 * masked_score, jnp.exp(s - top), 0.0)
                    total = alpha * jnp.where(kb == 0, 0.0, totals[h, rows])
                    totals[h, rows] = total + jnp.sum(p, axis=1, keepdims=True)
                    acc[h, rows] = alpha * jnp.where(kb == 0, 0.0, acc[h, rows])
                else:
                    p = jnp.exp(s - top)
                    sums.append(jnp.sum(p, axis=1, keepdims=True))
                weights[slot, rows] = p.astype(bf16)
            o = matmul(weights[slot], vals[:, cols])
            if blocks > 1:
                acc[h] = acc[h] + o
                ctx_ref[:, cols] = (acc[h] * (1.0 / jnp.maximum(totals[h], 1e-30))).astype(bf16)
            else:
                for r in range(tokens // tall):
                    rows = slice(r * tall, (r + 1) * tall)
                    ctx_ref[rows, cols] = (o[rows] * (1.0 / sums[r])).astype(bf16)
        return carry

    if blocks == 1:
        one_block(0, 0)
    else:
        lax.fori_loop(0, blocks, one_block, 0)


def exchange(x, ways):
    out = [x]
    for k in range(1, ways):
        low = k & -k
        source = out[k ^ low] if k != low else x
        out.append(lax.ppermute(source, "mp", [(i, i ^ low) for i in range(ways)]))
    return out


def body(
    patches,
    clip_of,
    owner_of,
    cites,
    latent_init,
    w_query,
    w_key,
    w_value,
    w_out,
    wx_key,
    wx_value,
    queries,
):
    groups = lax.axis_size("seq")
    ways = lax.axis_size("mp")
    clip_total = owner_of.shape[0]
    rows, wide = patches.shape
    width = w_query.shape[1]
    heads = width // RHD

    w_parts = exchange(w_out, ways)

    vmem = pl.BlockSpec(memory_space=pltpu.VMEM)
    smem = pl.BlockSpec(memory_space=pltpu.SMEM)
    anywhere = pl.BlockSpec(memory_space=pl.ANY)
    limit = lambda mib: pltpu.CompilerParams(vmem_limit_bytes=mib << 20)
    chunk = min(8, clip_total)
    pieces = 4
    wq, wk, wv = w_query.T, w_key.T, w_value.T
    packed, query_rows = pl.pallas_call(
        partial_kernel,
        in_specs=[smem, vmem, vmem] + [pl.BlockSpec(memory_space=pltpu.HBM)] * 4,
        out_specs=[vmem, vmem],
        scratch_shapes=[
            pltpu.VMEM((rows, wide), bf16),
            pltpu.VMEM((width, wide), bf16),
            pltpu.VMEM((width, wide), bf16),
            pltpu.VMEM((width, wide), bf16),
            pltpu.SemaphoreType.DMA((3 + pieces,)),
            pltpu.VMEM((heads * LAT, rows), f32),
            pltpu.VMEM((width, rows), bf16),
            pltpu.VMEM((heads, chunk * LAT, rows), bf16),
            pltpu.VMEM((heads * LAT, 128), f32),
            pltpu.VMEM((heads * LAT, 128), f32),
            pltpu.VMEM((3, 128, heads * LAT), f32),
        ],
        out_shape=[
            jax.ShapeDtypeStruct((groups, 176, 128), bf16),
            jax.ShapeDtypeStruct((heads * LAT, width), bf16),
        ],
        compiler_params=limit(32),
        name="partials",
    )(owner_of, clip_of.reshape(1, rows), latent_init, patches, wq, wk, wv)

    got = lax.all_to_all(packed, "seq", split_axis=0, concat_axis=0, tiled=True)

    lat_part = pl.pallas_call(
        latent_kernel,
        in_specs=[vmem] * 4,
        out_specs=vmem,
        out_shape=jax.ShapeDtypeStruct((168, 128), f32),
        compiler_params=limit(8),
        name="latents",
    )(latent_init, query_rows, wk, wv)

    spread = pl.pallas_call(
        merge_kernel,
        in_specs=[vmem] * 2,
        out_specs=vmem,
        out_shape=jax.ShapeDtypeStruct((groups, 160, 128), bf16),
        compiler_params=limit(16),
        name="merge",
    )(got, lat_part)

    everyone = lax.all_to_all(spread, "seq", split_axis=0, concat_axis=0, tiled=True)
    mixes = exchange(everyone, ways)

    cite_hot = cites[:, :, None] == jnp.arange(clip_total, dtype=jnp.int32)[None, None, :]
    cite_owner = jnp.sum(cite_hot * owner_of[None, None, :], axis=2)
    flags = -(-groups // 128) * 128
    cited = jnp.any(
        cite_owner[:, :, None] == jnp.arange(flags, dtype=jnp.int32)[None, None, :], axis=1
    ).astype(bf16)

    tokens, cross = queries.shape
    blocks = groups * LAT // KEYS
    scratch = [
        pltpu.VMEM((KEYS, wide), bf16),
        pltpu.VMEM((tokens, KEYS), f32),
        pltpu.VMEM((KEYS, cross), bf16),
        pltpu.VMEM((KEYS, cross), bf16),
        pltpu.VMEM((2, tokens, KEYS), f32),
        pltpu.VMEM((2, tokens, KEYS), bf16),
    ]
    init = latent_init
    if blocks == 1 and ways == 4 and KEYS > LAT:
        init = pl.pallas_call(
            begin_kernel,
            in_specs=[vmem] * 5,
            out_specs=vmem,
            out_shape=pltpu.VMEM((KEYS, wide), f32),
            compiler_params=limit(16),
            name="begin",
        )(mixes[0], mixes[1], w_parts[0], w_parts[1], latent_init)
        mixes, w_parts = mixes[2:], w_parts[2:]
    if blocks > 1:
        scratch += [
            pltpu.VMEM((cross // HD, tokens, HD), f32),
            pltpu.VMEM((cross // HD, tokens, 1), f32),
            pltpu.VMEM((cross // HD, tokens, 1), f32),
        ]
    resampled, context = pl.pallas_call(
        functools.partial(cross_kernel, blocks=blocks, ways=len(mixes)),
        in_specs=[smem] + [vmem] * (2 * len(mixes) + 5),
        out_specs=[vmem] * 2,
        scratch_shapes=scratch,
        out_shape=[
            jax.ShapeDtypeStruct((LAT, wide), bf16),
            jax.ShapeDtypeStruct((tokens, cross), bf16),
        ],
        compiler_params=limit(28),
        name="cross",
    )(
        lax.axis_index("seq").astype(jnp.int32).reshape(1),
        *mixes,
        *w_parts,
        init,
        cited,
        queries,
        wx_key,
        wx_value,
    )
    return (resampled, context)


def solution(mesh):
    in_specs = (
        P("seq", None),
        P("seq", None),
        P(),
        P("seq", None),
        P(),
        P(None, "mp"),
        P(None, "mp"),
        P(None, "mp"),
        P("mp", None),
        P(None, "mp"),
        P(None, "mp"),
        P("seq", "mp"),
    )
    out_specs = (P("seq", None), P("seq", "mp"))
    return jax.shard_map(body, mesh=mesh, in_specs=in_specs, out_specs=out_specs, check_vma=False)
```
